256 devices in a mesh: module: 4 (over y_lo, core), sample: 64 (over x, y_hi, z).
Axes of the slice: x: 4, y: 4 (y_hi: 2, y_lo: 2; y = y_hi * 2 + y_lo), z: 8, core: 2. Of those that a mesh axis runs over, the one named last changes fastest.
Arguments:
- queries: bfloat16 [16, 256, 4096], P('module', None, 'sample'), may hold values from -6 to 6
- inverse_hessian: bfloat16 [16, 4096, 4096], P('module', 'sample'), may hold values from -1 to 2.1, as said below
- train_grads: bfloat16 [16, 20480, 4096], P('module', 'sample'), may hold values from -0.09375 to 0.09375
Outputs:
- scores: float32 [20480, 256], P('sample')
The draws below stay inside these ranges and needn't reach their ends.
Inputs may be any that keep to these rules, and one draw needn't show every extreme that they name: `inverse_hessian`: each module's matrix is symmetric.
All inputs are finite; a program needn't handle non-finite values.
Results may differ from the reference program's by a relative error of at most 0.0029.
Values may be sent and summed in bfloat16 or wider, within the bound.
No kernel may reach another device: no remote copies, remote signals or barrier semaphores. Data moves between devices by JAX's collectives and lax.ppermute only.
A program may use at most 64 MiB of HBM per device.

```python
import math
import jax
import jax.numpy as jnp
from jax import lax

K = 4096
Q = 256
M = 16
S = 20480


def draw_inverse_hessian(key, part):
    noise_key = jax.random.fold_in(key, 11)
    diag_key = jax.random.fold_in(key, 12)
    noise = jax.random.normal(noise_key, (M, K, K), jnp.float32)
    lower, upper = (math.log(0.5), math.log(2.0))
    symmetric = (noise + jnp.swapaxes(noise, 1, 2)) * (0.35 * K ** (-0.5))
    diag_vals = jnp.exp(jax.random.uniform(diag_key, (M, K), jnp.float32, lower, upper))
    ident = jnp.eye(K, dtype=jnp.float32)
    return (symmetric + diag_vals[:, :, None] * ident[None, :, :]).astype(jnp.bfloat16)


def levels(key, dims, pieces, low, largest):
    gain, own = 1.0, jax.random.fold_in(key, 6)
    for position, shards_of in pieces:
        draws = jnp.exp(jax.random.uniform(jax.random.fold_in(own, position), (shards_of,), jnp.float32, low / len(pieces), largest / len(pieces)))
        gain = gain * jnp.repeat(draws, dims[position] // shards_of).reshape([-1 if axis == position else 1 for axis in range(len(dims))])
    return gain


def bell_draw(key, extent, scale, limit, shards=(), kind=jnp.bfloat16):
    drawn = jax.random.normal(key, extent, jnp.float32) * scale
    if len(shards) > 0:
        drawn = levels(key, extent, shards, -0.22, 0.18) * drawn
    return jnp.clip(drawn, min=-limit, max=limit).astype(kind)


def setup_inputs(seed: int = 0) -> dict:
    keys = jax.random.split(jax.random.key(seed), 4)
    queries = bell_draw(keys[0], (M, Q, K), 1.0, 6.0, ((0, 4), (2, 64)))
    inverse_hessian = draw_inverse_hessian(jax.random.fold_in(keys[3], 71), 0)
    train_grads = bell_draw(keys[2], (M, S, K), K ** -0.5, 0.09375, ((0, 4), (1, 64)))
    return dict(queries=queries, inverse_hessian=inverse_hessian, train_grads=train_grads)


def reference(queries, inverse_hessian, train_grads):
    def add_module(index, total):
        query = queries[index]
        matrix = inverse_hessian[index]
        grads = train_grads[index]
        precond = jnp.dot(query, matrix, preferred_element_type=jnp.float32).astype(jnp.bfloat16)
        return total + lax.dot_general(grads, precond, (((1,), (1,)), ((), ())), preferred_element_type=jnp.float32)

    start = jnp.zeros((train_grads.shape[1], queries.shape[1]), jnp.float32)
    return lax.fori_loop(0, queries.shape[0], add_module, start)
```

```python
import functools

import jax
import jax.numpy as jnp
from jax import lax
from jax.experimental import pallas as pl
from jax.experimental.pallas import tpu as pltpu
from jax.sharding import Mesh
from jax.sharding import PartitionSpec as P

X, Y, Z = "sample_0", "sample_1", "sample_2"
SAMPLE = (X, Y, Z)

OFFSETS = (0, 3, 1, 2)
SPLIT = 32


def shift(value, axis, step):
    size = lax.axis_size(axis)
    return lax.ppermute(value, axis, [(i, (i + step) % size) for i in range(size)])


def from_others(value):
    return [shift(value, X, 1), shift(value, X, -1), shift(value, X, 2)]


def ring(value, half):
    ahead, back = [value], [value]
    for _ in range(3):
        ahead.append(shift(ahead[-1], Z, 1))
        back.append(shift(back[-1], Z, -1))
    last_ahead = shift(ahead[-1][:half], Z, 1)
    last_back = shift(back[-1][half:], Z, -1)
    return ahead[1:], back[1:], last_ahead, last_back


def spot(plan, position):
    x, y, z = position
    dx, dy, dz = plan
    return lax.rem(x + OFFSETS[dx], 4), lax.rem(y + dy, 2), lax.rem(z + dz + 8, 8)


def precond_kernel(plans, own_ref, *refs):
    others, pieces = refs[:3], refs[3 : 3 + len(plans)]
    out_ref, slab, query, sems = refs[3 + len(plans) :]
    position = [lax.axis_index(a) for a in SAMPLE]
    for k, source in enumerate((own_ref.at[position[0]], *others)):
        x = lax.rem(position[0] + OFFSETS[k], 4)
        pltpu.make_async_copy(source, slab.at[x], sems.at[0]).start()
    for piece, parts in zip(pieces, plans):
        for index, plan in parts:
            x, y, z = spot(plan, position)
            pltpu.make_async_copy(piece.at[index], query.at[x, y, z], sems.at[1]).start()
    pltpu.make_async_copy(slab, slab, sems.at[0]).wait()
    pltpu.make_async_copy(query, query, sems.at[1]).wait()
    total = jnp.zeros((256, 256), jnp.float32)
    for x in range(4):
        total += jnp.dot(
            slab[:, :, x * 1024 : (x + 1) * 1024].reshape(256, 1024),
            query[x].reshape(1024, 256),
            preferred_element_type=jnp.float32,
        )
    out_ref[...] = total.reshape(4, 64, 256).astype(jnp.bfloat16)


def precondition(hessian, others, pieces, plans):
    return pl.pallas_call(
        functools.partial(precond_kernel, plans),
        out_shape=jax.ShapeDtypeStruct((4, 64, 256), jnp.bfloat16),
        in_specs=[pl.BlockSpec(memory_space=pl.ANY)] * (4 + len(pieces)),
        out_specs=pl.BlockSpec(memory_space=pltpu.VMEM),
        scratch_shapes=[
            pltpu.VMEM((4, 64, 4096), jnp.bfloat16),
            pltpu.VMEM((4, 2, 8, 64, 256), jnp.bfloat16),
            pltpu.SemaphoreType.DMA((2,)),
        ],
        cost_estimate=pl.CostEstimate(flops=2 * 256 * 4096 * 256, bytes_accessed=4 << 20, transcendentals=0),
        name="precond",
    )(hessian, *others, *pieces)


def scores_kernel(plans, grads_ref, *refs):
    pieces = refs[: len(plans)]
    out_ref, grads, precond, sems = refs[len(plans) :]
    position = [lax.axis_index(a) for a in SAMPLE]
    for k in range(4):
        m = lax.rem(position[0] + OFFSETS[k], 4)
        pltpu.make_async_copy(grads_ref.at[m], grads.at[k], sems.at[0, k]).start()
        for piece, parts in zip(pieces, plans):
            for index, plan, first, rows in parts:
                if plan[0] == k:
                    _, y, z = spot(plan, position)
                    target = precond.at[k, :, y, z, pl.ds(first, rows)]
                    pltpu.make_async_copy(piece.at[index], target, sems.at[1, k]).start()
    total = jnp.zeros(out_ref.shape, jnp.float32)
    for k in range(4):
        pltpu.make_async_copy(grads.at[k], grads.at[k], sems.at[0, k]).wait()
        pltpu.make_async_copy(precond.at[k], precond.at[k], sems.at[1, k]).wait()
        for x in range(4):
            total += jnp.dot(
                grads[k, :, x * 1024 : (x + 1) * 1024],
                precond[k, x].reshape(1024, 256),
                preferred_element_type=jnp.float32,
            )
    out_ref[...] = total


def scores_of(grads, pieces, plans):
    return pl.pallas_call(
        functools.partial(scores_kernel, plans),
        out_shape=jax.ShapeDtypeStruct((320, 256), jnp.float32),
        in_specs=[pl.BlockSpec(memory_space=pl.ANY)] * (1 + len(pieces)),
        out_specs=pl.BlockSpec(memory_space=pltpu.VMEM),
        scratch_shapes=[
            pltpu.VMEM((4, 320, 4096), jnp.bfloat16),
            pltpu.VMEM((4, 4, 2, 8, 64, 256), jnp.bfloat16),
            pltpu.SemaphoreType.DMA((2, 4)),
        ],
        cost_estimate=pl.CostEstimate(flops=2 * 320 * 16384 * 256, bytes_accessed=20 << 20, transcendentals=0),
        name="scores",
    )(grads, *pieces)


def with_others(mine, others):
    return jnp.stack([mine, *others])


def gather_queries(query):
    x = lax.axis_index(X)
    pick = lambda d: lax.dynamic_index_in_dim(query, lax.rem(x + d, 4), 0, False)
    mine = with_others(pick(0), [shift(pick(1), X, 1), shift(pick(3), X, -1), shift(pick(2), X, 2)])
    ahead, back, last_ahead, last_back = ring(mine, 2)
    last = jnp.concatenate([last_ahead, last_back])
    groups = [(mine[None], (0,))]
    for t in range(3):
        groups.append((jnp.stack([ahead[t], back[t]]), (-t - 1, t + 1)))
    groups.append((last[None], (4,)))
    pieces, plans = [], []
    for stack, offsets in groups:
        for dy, piece in enumerate((stack, shift(stack, Y, 1))):
            pieces.append(piece)
            plans.append([((n, dx), (dx, dy, dz)) for n, dz in enumerate(offsets) for dx in range(4)])
    return pieces, plans


def gather_precond(block):
    both = jnp.stack([block, shift(block, Y, 1)])
    column = [both, *from_others(both)]
    a = jnp.stack([c[:, :, :SPLIT] for c in column])
    b = both[:, :, SPLIT:]
    rest = 64 - SPLIT
    pieces, plans = [], []

    def add(piece, parts):
        pieces.append(piece)
        plans.append(parts)

    for dx, piece in enumerate(column):
        add(piece, [((dy,), (dx, dy, 0), 0, 64) for dy in range(2)])
    ahead, back, last_ahead, last_back = ring(b, 1)
    first = jnp.stack([ahead[0], back[0], ahead[1], back[1]])
    second = jnp.stack([ahead[2], back[2], jnp.concatenate([last_ahead, last_back])])
    for stack, offsets in ((first, (-1, 1, -2, 2)), (second, (-3, 3, 4))):
        for dx, piece in enumerate([stack, *from_others(stack)]):
            add(piece, [((n, dy), (dx, dy, dz), SPLIT, rest) for n, dz in enumerate(offsets) for dy in range(2)])
    ahead, back, last_ahead, last_back = ring(a, 2)
    for t in range(3):
        for piece, dz in ((ahead[t], -t - 1), (back[t], t + 1)):
            add(piece, [((dx, dy), (dx, dy, dz), 0, SPLIT) for dx in range(4) for dy in range(2)])
    for piece, base in ((last_ahead, 0), (last_back, 2)):
        add(piece, [((n, dy), (base + n, dy, 4), 0, SPLIT) for n in range(2) for dy in range(2)])
    return pieces, plans


def over_modules(scores):
    swap = [(0, 1), (1, 0), (2, 3), (3, 2)]
    chips = [(0, 2), (2, 0), (1, 3), (3, 1)]
    core = lax.rem(lax.axis_index("module"), 2)
    halves = scores.reshape(2, 160, 256)
    mine = lax.dynamic_index_in_dim(halves, core, 0, False)
    other = lax.dynamic_index_in_dim(halves, 1 - core, 0, False)
    mine = mine + lax.ppermute(other, "module", swap)
    mine = mine + lax.ppermute(mine, "module", chips)
    theirs = lax.ppermute(mine, "module", swap)
    first = core == 0
    return jnp.concatenate([jnp.where(first, mine, theirs), jnp.where(first, theirs, mine)])


def on_device(queries, inverse_hessian, train_grads):
    x = lax.axis_index(X)
    pick = lambda d: lax.dynamic_index_in_dim(inverse_hessian, lax.rem(x + d, 4), 0, False)
    rows = [shift(pick(1), X, 1), shift(pick(3), X, -1), shift(pick(2), X, 2)]
    pieces, plans = gather_queries(queries.transpose(0, 2, 1))
    block = precondition(inverse_hessian, rows, pieces, plans)
    pieces, plans = gather_precond(block)
    return over_modules(scores_of(train_grads, pieces, plans))


def solution(mesh):
    torus = Mesh(
        mesh.devices.reshape(mesh.shape["module"], 4, 2, 8),
        ("module", X, Y, Z),
    )
    in_specs = (P("module", None, SAMPLE), P("module", SAMPLE, None), P("module", SAMPLE, None))
    return jax.shard_map(
        on_device, mesh=torus, in_specs=in_specs, out_specs=P(SAMPLE, None), check_vma=False
    )
```
